1024 devices in a mesh: section: 64 (over x, y), tensor: 16 (over z, core).
Axes of the slice: x: 8, y: 8, z: 8, core: 2. Of those that a mesh axis runs over, the one named last changes fastest.
Arguments:
- vision_states: bfloat16 [256, 8192], P('section', 'tensor'), may hold values from -6 to 6
- projection: bfloat16 [64, 8192, 2, 2, 128], P('section', 'tensor'), may hold values from -0.0625 to 0.0625
- queries: bfloat16 [64, 2048, 2048], P('section', None, 'tensor'), may hold values from -400 to 400
- cotangent: bfloat16 [64, 2048, 2048], P('section', None, 'tensor'), may hold values from -6 to 6
- gate_logit: float32 [16], replicated, may hold values from 0.3 to 1.5
- tile_counts: int32 [2], replicated, may hold values from 1 to 4, as said below
Outputs:
- attended: bfloat16 [64, 2048, 2048], P('section', None, 'tensor')
- query_grad: bfloat16 [64, 2048, 2048], P('section', None, 'tensor')
- image_grad: float32 [256, 8192], P('section', 'tensor')
The draws below stay inside these ranges and needn't reach their ends.
Inputs may be any that keep to these rules, and one draw needn't show every extreme that they name: `tile_counts`: some sample has all 4 tiles and some sample has fewer.
All inputs are finite; a program needn't handle non-finite values.
Results may differ from the reference program's by a relative error of at most 0.025.
The reference program's roundings to bfloat16 on the way count: a program that leaves them out, or rounds other values in their place, can miss the bound.
Values may be sent and summed in bfloat16 or wider, within the bound.
A program may use at most 32 MiB of HBM per device.

```python
import jax
import jax.numpy as jnp
from jax import lax

D = 8192
HEADS = 64
KV_HEADS = 8
HEAD_DIM = 128
GROUPS = 4
SAMPLES = 2
SAMPLE_TOK = 1024
TILES = 4
TILE_ROWS = 32
TOK = 2048
IMG = 256
LAYERS = 16
KV_GROUP = 2
N_TENSOR = 16


def draw_queries(key, part):
    base_key = jax.random.fold_in(key, 0)
    shape_full = (LAYERS * GROUPS, TOK, HEADS // GROUPS * HEAD_DIM)
    values = jax.random.normal(base_key, shape_full, jnp.float32)
    values = jnp.clip(values, -400.0, 400.0)
    return values.astype(jnp.bfloat16)


def draw_tile_counts(key, part):
    first_key, second_key = jax.random.split(jax.random.fold_in(key, 7))
    counts = jax.random.randint(first_key, (SAMPLES,), 1, TILES)
    chosen = jax.random.randint(second_key, (), 0, SAMPLES)
    return jnp.where(jnp.arange(SAMPLES) == chosen, TILES, counts).astype(jnp.int32)


def level_of(key, shape, shards, low, top_value):
    def one(axis_at, blocks):
        heights = jax.random.uniform(jax.random.fold_in(jax.random.fold_in(key, 6), axis_at), (blocks,), jnp.float32, low / len(shards), top_value / len(shards))
        return jnp.repeat(jnp.exp(heights), shape[axis_at] // blocks).reshape((-1,) + (1,) * (len(shape) - axis_at - 1))

    level = one(*shards[0])
    for cut in shards[1:]:
        level = level * one(*cut)
    return level


def bell_draw(key, shape, scale, limit, shards=(), dtype=jnp.bfloat16):
    values = jax.random.normal(key, shape, jnp.float32) * scale
    if len(shards) > 0:
        values = level_of(key, shape, shards, -0.22, 0.18) * values
    return jnp.clip(values, min=-limit, max=limit).astype(dtype)


def setup_inputs(seed: int = 0) -> dict:
    key_list = jax.random.split(jax.random.key(seed), 7)
    return {
        "vision_states": bell_draw(key_list[0], (IMG, D), 1.0, 6.0, ((0, 64), (1, 16))),
        "projection": bell_draw(key_list[1], (LAYERS * GROUPS, D, KV_GROUP, 2, HEAD_DIM), D ** -0.5, 0.0625, ((0, 64), (1, 16))),
        "queries": draw_queries(jax.random.fold_in(key_list[6], 71), 0),
        "cotangent": bell_draw(key_list[3], (LAYERS * GROUPS, TOK, HEADS // GROUPS * HEAD_DIM), 1.0, 6.0, ((0, 64), (2, 16))),
        "gate_logit": jnp.clip(jax.random.uniform(key_list[4], (LAYERS,), jnp.float32, 0.3, 1.5), 0.3, 1.5),
        "tile_counts": draw_tile_counts(jax.random.fold_in(key_list[6], 71), 0),
    }


def reference(vision_states, projection, queries, cotangent, gate_logit, tile_counts):
    image_per = TILES * TILE_ROWS
    group_size = HEADS // KV_HEADS
    kv_local = KV_HEADS // GROUPS
    block_heads = HEADS // (GROUPS * N_TENSOR)
    sub_heads = min(block_heads, group_size)
    positions = lax.broadcasted_iota(jnp.int32, (SAMPLES, image_per), 1)
    usable = (positions < (tile_counts * TILE_ROWS)[:, None])[:, None, None, None, :]
    score_scale = HEAD_DIM ** -0.5
    gates = jnp.repeat(gate_logit, GROUPS)

    def one_layer(running, layer_inputs):
        weight, query_layer, cot_layer, logit = layer_inputs
        flat_weight = weight.reshape(D, kv_local * 2 * HEAD_DIM)
        key_values = jnp.dot(vision_states, flat_weight, preferred_element_type=jnp.float32).astype(jnp.bfloat16)
        key_values = key_values.reshape(SAMPLES, image_per, kv_local, 2, HEAD_DIM)
        keys_rows = key_values[:, :, :, 0].astype(jnp.float32)
        values_rows = key_values[:, :, :, 1].astype(jnp.float32)
        query_heads = query_layer.reshape(SAMPLES, SAMPLE_TOK, kv_local, group_size, HEAD_DIM).astype(jnp.float32)
        scores = jnp.einsum('bikgd,bjkd->bkgij', query_heads, keys_rows) * score_scale
        masked = jnp.where(usable, scores, -1e30)
        row_max = jnp.max(masked, axis=-1, keepdims=True)
        weights = jnp.where(usable, jnp.exp(masked - row_max), 0.0)
        probabilities = weights / jnp.sum(weights, axis=-1, keepdims=True)
        probs_low = probabilities.astype(jnp.bfloat16).astype(jnp.float32)
        gate_value = jnp.tanh(logit)
        combined = jnp.einsum('bkgij,bjkd->bikgd', probs_low, values_rows)
        attended = (gate_value * combined).astype(jnp.bfloat16).reshape(TOK, (HEADS // GROUPS) * HEAD_DIM)
        grad_input = (gate_value * cot_layer.astype(jnp.float32)).astype(jnp.bfloat16)
        grad_input = grad_input.reshape(SAMPLES, SAMPLE_TOK, kv_local, group_size, HEAD_DIM).astype(jnp.float32)
        grad_probs = jnp.einsum('bikgd,bjkd->bkgij', grad_input, values_rows)
        center = jnp.sum(probabilities * grad_probs, axis=-1, keepdims=True)
        grad_scores = (probabilities * (grad_probs - center)).astype(jnp.bfloat16).astype(jnp.float32)
        query_grad = jnp.einsum('bkgij,bjkd->bikgd', grad_scores, keys_rows) * score_scale
        query_grad = query_grad.astype(jnp.bfloat16).reshape(TOK, (HEADS // GROUPS) * HEAD_DIM)
        key_grad = jnp.einsum('bkgij,bikgd->bjkgd', grad_scores, query_heads) * score_scale
        value_grad = jnp.einsum('bkgij,bikgd->bjkgd', probs_low, grad_input)
        both_grads = jnp.stack([key_grad, value_grad], axis=4)
        both_grads = both_grads.reshape(SAMPLES, image_per, kv_local, group_size // sub_heads, sub_heads, 2, HEAD_DIM)
        block_sums = jnp.sum(both_grads, axis=4)
        rounded = lax.optimization_barrier(block_sums.astype(jnp.bfloat16)).astype(jnp.float32)
        head_sums = jnp.sum(rounded, axis=3).reshape(IMG, kv_local * 2 * HEAD_DIM)
        grad_layer = jnp.dot(head_sums, flat_weight.astype(jnp.float32).T, precision=lax.Precision.HIGHEST)
        return running + grad_layer, (attended, query_grad)

    initial = jnp.zeros((IMG, D), jnp.float32)
    running, outputs = lax.scan(one_layer, initial, (projection, queries, cotangent, gates))
    return outputs[0], outputs[1], running
```

```python
import jax
import jax.numpy as jnp
from jax import lax
from jax.experimental import pallas as pl
from jax.experimental.pallas import tpu as pltpu
from jax.sharding import PartitionSpec as P

MESH = pl.DeviceIdType.MESH
BF16 = jnp.bfloat16
F32 = jnp.float32

HEAD_DIM = 128
GROUPS = 4
TILE_ROWS = 32
TILES = 4
SCALE = HEAD_DIM ** (-0.5)
TOK = 2048
SAMPLE_TOK = 1024
CHUNK = 512
SIDE = 8


def arrived(ref, sem):
    pltpu.make_async_copy(ref, ref, sem).wait()


def kernel(
    vis_ref, w_ref, q_ref, cot_ref, gate_ref, count_ref,
    att_ref, qg_ref, img_ref,
    msg_f, msg, vin, vf, vb, w_raw, w_f, w_cat, w_t,
    q_v, cot_v, gi_v, q_t, gi_t, probs_s, ds_s,
    part, r1, kv, grads, r2, r3, g_f, e_msg, r4, att_v, qg_v,
    load_sem, w_send, w_recv, a_send, a_recv, b1_send, b1_recv, b2_send, b2_recv,
    d1_send, d1_recv, d2_send, d2_recv, e_send, e_recv, out_sem,
):
    sec = lax.axis_index("section")
    ten = lax.axis_index("tensor")
    x, y = sec // SIDE, sec % SIDE
    z, core = ten // 2, ten % 2
    sample = x // 4
    half = z // 4
    tile = z % 4
    slot = ten % 8
    is_own = core == sample

    def tensor_peer(t):
        return (sec, t)

    load_q = pltpu.make_async_copy(q_ref, q_v, load_sem.at[0])
    load_c = pltpu.make_async_copy(cot_ref, cot_v, load_sem.at[1])
    load_w = pltpu.make_async_copy(w_ref, w_raw.at[core], load_sem.at[2])
    load_w.start()
    load_c.start()
    load_q.start()

    barrier = pltpu.get_barrier_semaphore()

    def greet_plane(i, carry):
        tx = 4 * core + (i // 16)
        ty = (i // 2) % SIDE
        m = i % 2
        me = jnp.logical_and(jnp.logical_and(tx == x, ty == y), m == core)

        @pl.when(jnp.logical_not(me))
        def _():
            pl.semaphore_signal(
                barrier, inc=1, device_id=(tx * SIDE + ty, z * 2 + m), device_id_type=MESH
            )

        return carry

    def greet_line(i, carry):
        pl.semaphore_signal(
            barrier, inc=1, device_id=tensor_peer(half * 8 + (slot + i) % 8), device_id_type=MESH
        )
        return carry

    def greet_far(i, carry):
        pl.semaphore_signal(
            barrier, inc=1, device_id=tensor_peer(((1 - half) * 4 + i) * 2 + core),
            device_id_type=MESH,
        )
        return carry

    lax.fori_loop(0, 64, greet_plane, 0)
    lax.fori_loop(1, 8, greet_line, 0)
    lax.fori_loop(0, 4, greet_far, 0)

    for k in range(4):
        msg_f[4 * k : 4 * k + 4, :] = vis_ref[:, 128 * k : 128 * (k + 1)].astype(F32)
    msg[...] = msg_f[...].astype(BF16)

    pl.semaphore_wait(barrier, 75 - is_own.astype(jnp.int32))

    a_slot = (x % 4) * 16 + y * 2 + core

    def a_copy(i):
        tx = (x + 4 + i // SIDE) % SIDE
        ty = (y + 4 + i % SIDE) % SIDE
        me = jnp.logical_and(jnp.logical_and(tx == x, ty == y), is_own)
        return me, pltpu.make_async_remote_copy(
            src_ref=msg, dst_ref=vin.at[a_slot], send_sem=a_send, recv_sem=a_recv.at[x % 4],
            device_id=(tx * SIDE + ty, z * 2 + sample), device_id_type=MESH,
        )

    def a_start(i, carry):
        me, copy = a_copy(i)

        @pl.when(me)
        def _():
            pltpu.make_async_copy(msg, vin.at[a_slot], a_recv.at[x % 4]).start()

        @pl.when(jnp.logical_not(me))
        def _():
            copy.start()

        return carry

    lax.fori_loop(0, 64, a_start, 0)
    w_copy = pltpu.make_async_remote_copy(
        src_ref=w_ref, dst_ref=w_raw.at[core], send_sem=w_send, recv_sem=w_recv,
        device_id=tensor_peer(z * 2 + 1 - core), device_id_type=MESH,
    )
    w_copy.start()

    gate = jnp.tanh(jnp.full((8, 128), gate_ref[sec // GROUPS], F32))[0:1, 0:1]

    def lay_out(m):
        w_f[...] = w_raw[m].astype(F32)
        for n in range(4):
            block = w_f[pl.ds(n, 512, stride=4), :]
            w_cat[m, :, 128 * n : 128 * (n + 1)] = block.astype(BF16)
            w_t[m, 128 * n : 128 * (n + 1), :] = block.T.astype(BF16)

    load_w.wait()
    lay_out(core)
    w_copy.wait_recv()
    lay_out(1 - core)
    load_c.wait()
    load_q.wait()
    for t in range(TOK // CHUNK):
        rows = slice(t * CHUNK, (t + 1) * CHUNK)
        gi = (gate * cot_v[rows, :].astype(F32)).astype(BF16)
        gi_v[rows, :] = gi
        gi_t[:, rows] = gi.astype(F32).T.astype(BF16)
        q_t[:, rows] = q_v[rows, :].astype(F32).T.astype(BF16)

    def b1_copy(dest, source):
        return pltpu.make_async_remote_copy(
            src_ref=part.at[dest], dst_ref=r1.at[z], send_sem=b1_send, recv_sem=b1_recv,
            device_id=tensor_peer(dest * 2 + core), device_id_type=MESH,
        )

    for j in range(TILES):
        arrived(vin.at[pl.ds(16 * j, 16)], a_recv.at[j])
        vf[...] = vin[16 * j : 16 * (j + 1)].reshape(256, 128).astype(F32)
        for m in range(2):
            for k in range(4):
                rows = [vf[pl.ds(m * 16 + 4 * k + r, 8, stride=32), :] for r in range(4)]
                vb[m, :, 128 * k : 128 * (k + 1)] = jnp.concatenate(rows, axis=0).astype(BF16)
        total = jnp.dot(vb[0], w_cat[0], preferred_element_type=F32) + jnp.dot(
            vb[1], w_cat[1], preferred_element_type=F32
        )
        for g in range(2):
            dest = 4 * g + j
            part[dest] = total[:, 256 * g : 256 * (g + 1)]

            @pl.when(dest != z)
            def _():
                b1_copy(dest, j).start()

    arrived(r1.at[pl.ds(0, 7)], b1_recv)
    total = part[z]
    for i in range(1, 8):
        total = total + r1[(z + i) % 8]
    kv_slot = core * 4 + tile
    kv[kv_slot] = total.astype(BF16)

    def b2_start(i, carry):
        pltpu.make_async_remote_copy(
            src_ref=kv.at[kv_slot], dst_ref=kv.at[kv_slot], send_sem=b2_send, recv_sem=b2_recv,
            device_id=tensor_peer(half * 8 + (slot + i) % 8), device_id_type=MESH,
        ).start()
        return carry

    lax.fori_loop(1, 8, b2_start, 0)
    arrived(kv.at[pl.ds(0, 7)], b2_recv)

    row_tile = lax.broadcasted_iota(jnp.int32, (128, CHUNK), 0) // TILE_ROWS
    for b in range(2):
        both = kv[4 * b : 4 * b + 4].reshape(128, 256)
        keys, values = both[:, :128], both[:, 128:]
        usable = row_tile < count_ref[b]
        key_grad = jnp.zeros((128, HEAD_DIM), F32)
        value_grad = jnp.zeros((128, HEAD_DIM), F32)
        for t in range(SAMPLE_TOK // CHUNK):
            rows = slice(b * SAMPLE_TOK + t * CHUNK, b * SAMPLE_TOK + (t + 1) * CHUNK)
            scores = jnp.dot(keys, q_t[:, rows], preferred_element_type=F32) * SCALE
            masked = jnp.where(usable, scores, -1e30)
            row_max = jnp.max(masked, axis=0, keepdims=True)
            weights = jnp.where(usable, jnp.exp(masked - row_max), 0.0)
            probs = weights * (1.0 / jnp.sum(weights, axis=0, keepdims=True))
            probs_low = probs.astype(BF16)
            grad_probs = jnp.dot(values, gi_t[:, rows], preferred_element_type=F32)
            center = jnp.sum(probs * grad_probs, axis=0, keepdims=True)
            grad_scores = (probs * (grad_probs - center)).astype(BF16)
            key_grad = key_grad + jnp.dot(grad_scores, q_v[rows, :], preferred_element_type=F32)
            value_grad = value_grad + jnp.dot(probs_low, gi_v[rows, :], preferred_element_type=F32)
            probs_s[:, rows] = probs_low
            ds_s[:, rows] = grad_scores
        part_grads = jnp.concatenate([(key_grad * SCALE).astype(BF16), value_grad.astype(BF16)], axis=1)
        grads[4 * b : 4 * b + 4] = part_grads.reshape(4, 32, 256)

        for j in range(TILES):
            dest = j * 2 + b

            @pl.when(dest != slot)
            def _():
                pltpu.make_async_remote_copy(
                    src_ref=grads.at[4 * b + j], dst_ref=r2.at[slot],
                    send_sem=d1_send, recv_sem=d1_recv,
                    device_id=tensor_peer(half * 8 + dest), device_id_type=MESH,
                ).start()

    def outputs(b):
        both = kv[4 * b : 4 * b + 4].reshape(128, 256).astype(F32)
        keys_t, values_t = both[:, :128].T.astype(BF16), both[:, 128:].T.astype(BF16)
        for t in range(SAMPLE_TOK // CHUNK):
            rows = slice(b * SAMPLE_TOK + t * CHUNK, b * SAMPLE_TOK + (t + 1) * CHUNK)
            combined = jnp.dot(values_t, probs_s[:, rows], preferred_element_type=F32)
            att_v[rows, :] = (gate * combined).T.astype(BF16)
            query_grad = jnp.dot(keys_t, ds_s[:, rows], preferred_element_type=F32) * SCALE
            qg_v[rows, :] = query_grad.T.astype(BF16)

    outputs(0)
    arrived(r2.at[pl.ds(0, 7)], d1_recv)
    total = grads[kv_slot].astype(F32)
    for i in range(1, 8):
        total = total + r2[(slot + i) % 8].astype(F32)
    r3[z] = total.astype(BF16)

    def d2_start(i, carry):
        pltpu.make_async_remote_copy(
            src_ref=r3.at[z], dst_ref=r3.at[z], send_sem=d2_send, recv_sem=d2_recv,
            device_id=tensor_peer(((z + i) % 8) * 2 + core), device_id_type=MESH,
        ).start()
        return carry

    lax.fori_loop(1, 8, d2_start, 0)
    outputs(1)
    store_a = pltpu.make_async_copy(att_v, att_ref, out_sem.at[0])
    store_q = pltpu.make_async_copy(qg_v, qg_ref, out_sem.at[1])
    store_a.start()
    store_q.start()
    arrived(r3.at[pl.ds(0, 7)], d2_recv)

    sums = jnp.concatenate([r3[0:4].reshape(128, 256), r3[4:8].reshape(128, 256)], axis=1)
    for m in range(2):
        grad = jnp.dot(sums, w_t[m], preferred_element_type=F32)
        for j in range(TILES):
            for k in range(4):
                for r in range(4):
                    g_f[pl.ds(256 * j + 16 * m + 4 * k + r, 8, stride=32), :] = grad[
                        32 * j + 8 * r : 32 * j + 8 * (r + 1), 128 * k : 128 * (k + 1)
                    ]
    e_msg[...] = g_f[...].astype(BF16).reshape(64, 16, 128)

    def e_start(i, carry):
        j = (x + 2 + i // 16) % 4
        ty = (y + 4 + (i // 2) % SIDE) % SIDE
        m = i % 2
        tx = 4 * core + j
        source = e_msg.at[j * 16 + ty * 2 + m]
        me = jnp.logical_and(jnp.logical_and(tx == x, ty == y), m == core)

        @pl.when(me)
        def _():
            pltpu.make_async_copy(source, r4.at[sec], e_recv).start()

        @pl.when(jnp.logical_not(me))
        def _():
            pltpu.make_async_remote_copy(
                src_ref=source, dst_ref=r4.at[sec], send_sem=e_send, recv_sem=e_recv,
                device_id=(tx * SIDE + ty, z * 2 + m), device_id_type=MESH,
            ).start()

        return carry

    lax.fori_loop(0, 64, e_start, 0)

    w_copy.wait_send()
    arrived(part.at[pl.ds(0, 7)], b1_send)
    arrived(kv.at[pl.ds(0, 7)], b2_send)
    arrived(grads.at[pl.ds(0, 7)], d1_send)
    arrived(r3.at[pl.ds(0, 7)], d2_send)

    @pl.when(is_own)
    def _():
        arrived(vin.at[pl.ds(0, 63)], a_send)
        arrived(e_msg.at[pl.ds(0, 63)], e_send)

    @pl.when(jnp.logical_not(is_own))
    def _():
        arrived(vin, a_send)
        arrived(e_msg, e_send)

    arrived(r4, e_recv)
    image = jnp.sum(r4[...].astype(F32), axis=0)
    for k in range(4):
        img_ref[:, 128 * k : 128 * (k + 1)] = image[4 * k : 4 * k + 4, :]
    store_a.wait()
    store_q.wait()


def on_device(vision_states, projection, queries, cotangent, gate_logit, tile_counts):
    vmem = pl.BlockSpec(memory_space=pltpu.VMEM)
    smem = pl.BlockSpec(memory_space=pltpu.SMEM)
    hbm = pl.BlockSpec(memory_space=pl.ANY)
    dma = pltpu.SemaphoreType.DMA
    tile8 = pltpu.VMEM((8, 32, 256), BF16)
    tok = pltpu.VMEM((TOK, HEAD_DIM), BF16)
    tok_t = pltpu.VMEM((HEAD_DIM, TOK), BF16)
    blocks = pltpu.VMEM((64, 16, 128), BF16)
    attended, query_grad, image_grad = pl.pallas_call(
        kernel,
        out_shape=(
            jax.ShapeDtypeStruct((TOK, HEAD_DIM), BF16),
            jax.ShapeDtypeStruct((TOK, HEAD_DIM), BF16),
            jax.ShapeDtypeStruct((4, 512), F32),
        ),
        in_specs=[vmem, hbm, hbm, hbm, smem, smem],
        out_specs=(hbm, hbm, vmem),
        scratch_shapes=[
            pltpu.VMEM((16, 128), F32),
            pltpu.VMEM((16, 128), BF16),
            blocks,
            pltpu.VMEM((256, 128), F32),
            pltpu.VMEM((2, 32, 512), BF16),
            pltpu.VMEM((2, 2048, 128), BF16),
            pltpu.VMEM((2048, 128), F32),
            pltpu.VMEM((2, 512, 512), BF16),
            pltpu.VMEM((2, 512, 512), BF16),
            tok, tok, tok, tok_t, tok_t, tok_t, tok_t,
            pltpu.VMEM((8, 32, 256), F32),
            pltpu.VMEM((8, 32, 256), F32),
            tile8, tile8, tile8, tile8,
            pltpu.VMEM((1024, 128), F32),
            blocks, blocks,
            tok, tok,
            dma((3,)), dma, dma, dma, dma((4,)), dma, dma, dma, dma,
            dma, dma, dma, dma, dma, dma, dma((2,)),
        ],
        compiler_params=pltpu.CompilerParams(collective_id=0, has_side_effects=True),
        name="cross_attention",
    )(
        vision_states,
        projection.reshape(2048, 128),
        queries.reshape(TOK, HEAD_DIM),
        cotangent.reshape(TOK, HEAD_DIM),
        gate_logit,
        tile_counts,
    )
    return (
        attended.reshape(queries.shape),
        query_grad.reshape(queries.shape),
        image_grad,
    )


def solution(mesh):
    return jax.shard_map(
        on_device,
        mesh=mesh,
        in_specs=(
            P("section", "tensor"),
            P("section", "tensor", None, None, None),
            P("section", None, "tensor"),
            P("section", None, "tensor"),
            P(),
            P(),
        ),
        out_specs=(
            P("section", None, "tensor"),
            P("section", None, "tensor"),
            P("section", "tensor"),
        ),
        check_vma=False,
    )
```

```python
import jax
import jax.numpy as jnp
from jax import lax
from jax.experimental import pallas as pl
from jax.experimental.pallas import tpu as pltpu
from jax.sharding import PartitionSpec as P

MESH = pl.DeviceIdType.MESH
BF16 = jnp.bfloat16
F32 = jnp.float32

HEAD_DIM = 128
GROUPS = 4
TILE_ROWS = 32
TILES = 4
SCALE = HEAD_DIM ** (-0.5)
TOK = 2048
SAMPLE_TOK = 1024
CHUNK = 512
SIDE = 8
FAR_FIRST = (4, 3, 5, 2, 6, 1, 7)


def arrived(ref, sem):
    pltpu.make_async_copy(ref, ref, sem).wait()


def kernel(
    vis_ref, w_ref, q_ref, cot_ref, gate_ref, count_ref,
    att_ref, qg_ref, img_ref,
    gate_s, count_s, vis_v, msg_f, msg, vin_a, vin_b, vf, vb_a, vb_b, w_raw, w_f, w_cat, w_t,
    q_v, cot_v, gi_v, q_t, gi_t, probs_s, ds_s,
    part, r1, kv, grads, r2, r3, g_f, em_a, em_b, ea1, eb1, es_a, es_b, e2,
    load_sem, w_send, w_recv, a1_send, a1a_recv, a1b_recv, a2a_send, a2b_send, a2a_recv, a2b_recv,
    b1_send, b1_recv, b2_send, b2_recv, d1_send, d1_recv, d2_send, d2_recv,
    ea1_send, eb1_send, ea1_recv, eb1_recv, e2a_send, e2b_send, e2_recv,
):
    sec = lax.axis_index("section")
    ten = lax.axis_index("tensor")
    x, y = sec // SIDE, sec % SIDE
    z, core = ten // 2, ten % 2
    sample = x // 4
    half = z // 4
    tile = x % 4
    sum_tile = z % 4
    slot = ten % 8
    is_own = core == sample

    def chip(cx, cy, c):
        return (cx * SIDE + cy, z * 2 + c)

    def tensor_peer(t):
        return (sec, t)

    def remote(src, dst, send, recv, device):
        return pltpu.make_async_remote_copy(
            src_ref=src, dst_ref=dst, send_sem=send, recv_sem=recv,
            device_id=device, device_id_type=MESH,
        )

    load_v = pltpu.make_async_copy(vis_ref, vis_v, load_sem.at[3])
    load_q = pltpu.make_async_copy(q_ref, q_v, load_sem.at[0])
    load_c = pltpu.make_async_copy(cot_ref, cot_v, load_sem.at[1])
    load_w = pltpu.make_async_copy(w_ref, w_raw.at[core], load_sem.at[2])
    load_g = pltpu.make_async_copy(gate_ref, gate_s, load_sem.at[4])
    load_n = pltpu.make_async_copy(count_ref, count_s, load_sem.at[5])
    load_v.start()
    load_g.start()
    load_n.start()
    load_w.start()
    load_c.start()
    load_q.start()

    barrier = pltpu.get_barrier_semaphore()

    def greet(device):
        pl.semaphore_signal(barrier, inc=1, device_id=device, device_id_type=MESH)

    for d in FAR_FIRST:
        for c in range(2):
            greet(chip((x + d) % SIDE, y, c))
            greet(chip(x, (y + d) % SIDE, c))
    for i in range(1, 8):
        greet(tensor_peer(half * 8 + (slot + i) % 8))
    for i in range(4):
        greet(tensor_peer(((1 - half) * 4 + i) * 2 + core))

    load_v.wait()
    for k in range(4):
        msg_f[4 * k : 4 * k + 4, :] = vis_v[:, 128 * k : 128 * (k + 1)].astype(F32)
    msg[...] = msg_f[...].astype(BF16)

    pl.semaphore_wait(barrier, 39)

    @pl.when(core == 0)
    def _():
        for d in FAR_FIRST:
            remote(msg, vin_a.at[tile, y], a1_send, a1a_recv, chip(x, (y + d) % SIDE, sample)).start()

        @pl.when(is_own)
        def _():
            pltpu.make_async_copy(msg, vin_a.at[tile, y], a1a_recv).start()

        @pl.when(jnp.logical_not(is_own))
        def _():
            remote(msg, vin_a.at[tile, y], a1_send, a1a_recv, chip(x, y, 1)).start()

    @pl.when(core == 1)
    def _():
        for d in FAR_FIRST:
            remote(msg, vin_b.at[y, tile], a1_send, a1b_recv, chip((x + d) % SIDE, y, sample)).start()

        @pl.when(is_own)
        def _():
            pltpu.make_async_copy(msg, vin_b.at[y, tile], a1b_recv).start()

        @pl.when(jnp.logical_not(is_own))
        def _():
            remote(msg, vin_b.at[y, tile], a1_send, a1b_recv, chip(x, y, 0)).start()

    w_copy = remote(w_ref, w_raw.at[core], w_send, w_recv, tensor_peer(z * 2 + 1 - core))
    w_copy.start()

    def lay_out(m):
        w_f[...] = w_raw[m].astype(F32)
        for n in range(4):
            block = w_f[pl.ds(n, 512, stride=4), :]
            w_cat[m, :, 128 * n : 128 * (n + 1)] = block.astype(BF16)
            w_t[m, 128 * n : 128 * (n + 1), :] = block.T.astype(BF16)

    load_w.wait()
    lay_out(core)

    arrived(vin_b.at[y], a1b_recv)
    for d in FAR_FIRST:
        remote(vin_b.at[y], vin_b.at[y], a2b_send, a2b_recv, chip(x, (y + d) % SIDE, core)).start()

    @pl.when(is_own)
    def _():
        arrived(vin_a.at[tile], a1a_recv)
        for d in FAR_FIRST:
            remote(vin_a.at[tile], vin_a.at[tile], a2a_send, a2a_recv, chip((x + d) % SIDE, y, core)).start()

    load_g.wait()
    load_n.wait()
    gate = jnp.tanh(jnp.full((8, 128), gate_s[sec // GROUPS], F32))[0:1, 0:1]
    w_copy.wait_recv()
    lay_out(1 - core)
    load_c.wait()
    load_q.wait()
    for t in range(TOK // CHUNK):
        rows = slice(t * CHUNK, (t + 1) * CHUNK)
        gi = (gate * cot_v[rows, :].astype(F32)).astype(BF16)
        gi_v[rows, :] = gi
        gi_t[:, rows] = gi.astype(F32).T.astype(BF16)
        q_t[:, rows] = q_v[rows, :].astype(F32).T.astype(BF16)

    def rows_of(blocks, out):
        for j in range(TILES):
            vf[...] = blocks(j).reshape(128, 128).astype(F32)
            for k in range(4):
                rows = [vf[pl.ds(4 * k + r, 8, stride=16), :] for r in range(4)]
                out[32 * j : 32 * (j + 1), 128 * k : 128 * (k + 1)] = jnp.concatenate(
                    rows, axis=0
                ).astype(BF16)

    arrived(vin_b.at[pl.ds(0, 7)], a2b_recv)
    rows_of(lambda j: vin_b[:, j], vb_b)

    @pl.when(is_own)
    def _():
        arrived(vin_a.at[pl.ds(0, 3)], a2a_recv)

    @pl.when(jnp.logical_not(is_own))
    def _():
        arrived(vin_a, a2a_recv)

    rows_of(lambda j: vin_a[j], vb_a)
    total = jnp.dot(vb_a[...], w_cat[0], preferred_element_type=F32) + jnp.dot(
        vb_b[...], w_cat[1], preferred_element_type=F32
    )
    for g in range(2):
        part[4 * g : 4 * g + 4] = total[:, 256 * g : 256 * (g + 1)].reshape(4, 32, 256)
    for d in FAR_FIRST:
        dest = (z + d) % 8
        remote(part.at[dest], r1.at[z], b1_send, b1_recv, tensor_peer(dest * 2 + core)).start()

    arrived(r1.at[pl.ds(0, 7)], b1_recv)
    total = part[z]
    for i in range(1, 8):
        total = total + r1[(z + i) % 8]
    kv_slot = core * 4 + sum_tile
    kv[kv_slot] = total.astype(BF16)

    for i in range(1, 8):
        remote(
            kv.at[kv_slot], kv.at[kv_slot], b2_send, b2_recv,
            tensor_peer(half * 8 + (slot + i) % 8),
        ).start()
    arrived(kv.at[pl.ds(0, 7)], b2_recv)

    row_tile = lax.broadcasted_iota(jnp.int32, (128, CHUNK), 0) // TILE_ROWS
    for b in range(2):
        both = kv[4 * b : 4 * b + 4].reshape(128, 256)
        keys, values = both[:, :128], both[:, 128:]
        usable = row_tile < count_s[b]
        key_grad = jnp.zeros((128, HEAD_DIM), F32)
        value_grad = jnp.zeros((128, HEAD_DIM), F32)
        for t in range(SAMPLE_TOK // CHUNK):
            rows = slice(b * SAMPLE_TOK + t * CHUNK, b * SAMPLE_TOK + (t + 1) * CHUNK)
            scores = jnp.dot(keys, q_t[:, rows], preferred_element_type=F32) * SCALE
            masked = jnp.where(usable, scores, -1e30)
            row_max = jnp.max(masked, axis=0, keepdims=True)
            weights = jnp.where(usable, jnp.exp(masked - row_max), 0.0)
            probs = weights * (1.0 / jnp.sum(weights, axis=0, keepdims=True))
            probs_low = probs.astype(BF16)
            grad_probs = jnp.dot(values, gi_t[:, rows], preferred_element_type=F32)
            center = jnp.sum(probs * grad_probs, axis=0, keepdims=True)
            grad_scores = (probs * (grad_probs - center)).astype(BF16)
            key_grad = key_grad + jnp.dot(grad_scores, q_v[rows, :], preferred_element_type=F32)
            value_grad = value_grad + jnp.dot(probs_low, gi_v[rows, :], preferred_element_type=F32)
            probs_s[:, rows] = probs_low
            ds_s[:, rows] = grad_scores
        part_grads = jnp.concatenate([(key_grad * SCALE).astype(BF16), value_grad.astype(BF16)], axis=1)
        grads[4 * b : 4 * b + 4] = part_grads.reshape(4, 32, 256)

        for j in range(TILES):
            dest = j * 2 + b

            @pl.when(dest != slot)
            def _():
                remote(
                    grads.at[4 * b + j], r2.at[slot], d1_send, d1_recv, tensor_peer(half * 8 + dest)
                ).start()

    def outputs(b):
        both = kv[4 * b : 4 * b + 4].reshape(128, 256).astype(F32)
        keys_t, values_t = both[:, :128].T.astype(BF16), both[:, 128:].T.astype(BF16)
        for t in range(SAMPLE_TOK // CHUNK):
            rows = slice(b * SAMPLE_TOK + t * CHUNK, b * SAMPLE_TOK + (t + 1) * CHUNK)
            combined = jnp.dot(values_t, probs_s[:, rows], preferred_element_type=F32)
            att_ref[rows, :] = (gate * combined).T.astype(BF16)
            query_grad = jnp.dot(keys_t, ds_s[:, rows], preferred_element_type=F32) * SCALE
            qg_ref[rows, :] = query_grad.T.astype(BF16)

    outputs(0)
    arrived(r2.at[pl.ds(0, 7)], d1_recv)
    total = grads[kv_slot].astype(F32)
    for i in range(1, 8):
        total = total + r2[(slot + i) % 8].astype(F32)
    r3[z] = total.astype(BF16)

    for d in FAR_FIRST:
        remote(
            r3.at[z], r3.at[z], d2_send, d2_recv, tensor_peer(((z + d) % 8) * 2 + core)
        ).start()
    outputs(1)
    arrived(r3.at[pl.ds(0, 7)], d2_recv)

    sums = jnp.concatenate([r3[0:4].reshape(128, 256), r3[4:8].reshape(128, 256)], axis=1)

    def spread(m, where, step):
        grad = jnp.dot(sums, w_t[m], preferred_element_type=F32)
        for j in range(TILES):
            for k in range(4):
                for r in range(4):
                    g_f[m, pl.ds(where(j) + 4 * k + r, 8, stride=step), :] = grad[
                        32 * j + 8 * r : 32 * j + 8 * (r + 1), 128 * k : 128 * (k + 1)
                    ]
        return g_f[m].astype(BF16)

    em_b[...] = spread(1, lambda j: 16 * j, 64).reshape(8, 4, 16, 128)
    for d in FAR_FIRST:
        ty = (y + d) % SIDE
        remote(em_b.at[ty], eb1.at[y], eb1_send, eb1_recv, chip(x, ty, core)).start()
    em_a[...] = spread(0, lambda j: 128 * j, 16).reshape(4, 8, 16, 128)
    own_a = jnp.logical_and(core == 0, is_own)
    own_b = jnp.logical_and(core == 1, is_own)
    for i in range(4):
        j = (tile + 2 + i) % 4
        me = jnp.logical_and(own_a, j == tile)

        @pl.when(me)
        def _():
            pltpu.make_async_copy(em_a.at[j], ea1.at[x], ea1_recv).start()

        @pl.when(jnp.logical_not(me))
        def _():
            remote(em_a.at[j], ea1.at[x], ea1_send, ea1_recv, chip(4 * core + j, y, 0)).start()

    arrived(eb1.at[pl.ds(0, 7)], eb1_recv)
    total = em_b[y].astype(F32)
    for d in range(1, 8):
        total = total + eb1[(y + d) % 8].astype(F32)
    es_b[...] = total.astype(BF16)
    for i in range(4):
        j = (tile + 2 + i) % 4
        me = jnp.logical_and(own_b, j == tile)

        @pl.when(me)
        def _():
            pltpu.make_async_copy(es_b.at[j], e2.at[x], e2_recv).start()

        @pl.when(jnp.logical_not(me))
        def _():
            remote(es_b.at[j], e2.at[x], e2b_send, e2_recv, chip(4 * core + j, y, 1)).start()

    @pl.when(core == 0)
    def _():
        arrived(ea1, ea1_recv)
        total = ea1[0].astype(F32)
        for i in range(1, 8):
            total = total + ea1[i].astype(F32)
        es_a[...] = total.astype(BF16)
        for d in FAR_FIRST:
            ty = (y + d) % SIDE
            remote(es_a.at[ty], e2.at[y], e2a_send, e2_recv, chip(x, ty, 0)).start()
        e2[y] = es_a[y]

    w_copy.wait_send()
    arrived(vin_b.at[pl.ds(0, 7)], a2b_send)
    arrived(part.at[pl.ds(0, 7)], b1_send)
    arrived(kv.at[pl.ds(0, 7)], b2_send)
    arrived(grads.at[pl.ds(0, 7)], d1_send)
    arrived(r3.at[pl.ds(0, 7)], d2_send)
    arrived(em_b.at[pl.ds(0, 7)], eb1_send)

    @pl.when(is_own)
    def _():
        arrived(vin_a.at[0, pl.ds(0, 7)], a1_send)
        arrived(ea1.at[pl.ds(0, 7)], a2a_send)

    @pl.when(jnp.logical_not(is_own))
    def _():
        arrived(vin_a.at[0], a1_send)

    @pl.when(own_a)
    def _():
        arrived(em_a.at[pl.ds(0, 3)], ea1_send)

    @pl.when(jnp.logical_not(own_a))
    def _():
        arrived(em_a, ea1_send)

    @pl.when(own_b)
    def _():
        arrived(es_b.at[pl.ds(0, 3)], e2b_send)

    @pl.when(jnp.logical_not(own_b))
    def _():
        arrived(es_b, e2b_send)

    @pl.when(core == 0)
    def _():
        arrived(es_a.at[pl.ds(0, 7)], e2a_send)

    @pl.when(core == 0)
    def _():
        arrived(e2.at[pl.ds(0, 7)], e2_recv)

    @pl.when(core == 1)
    def _():
        arrived(e2, e2_recv)

    image = jnp.sum(e2[...].astype(F32), axis=0)
    for k in range(4):
        img_ref[:, 128 * k : 128 * (k + 1)] = image[4 * k : 4 * k + 4, :]


def on_device(vision_states, projection, queries, cotangent, gate_logit, tile_counts):
    vmem = pl.BlockSpec(memory_space=pltpu.VMEM)
    hbm = pl.BlockSpec(memory_space=pltpu.HBM)
    dma = pltpu.SemaphoreType.DMA
    tile8 = pltpu.VMEM((8, 32, 256), BF16)
    tok = pltpu.VMEM((TOK, HEAD_DIM), BF16)
    tok_t = pltpu.VMEM((HEAD_DIM, TOK), BF16)

    def blocks(*lead):
        return pltpu.VMEM((*lead, 16, 128), BF16)

    attended, query_grad, image_grad = pl.pallas_call(
        kernel,
        out_shape=(
            jax.ShapeDtypeStruct((TOK, HEAD_DIM), BF16),
            jax.ShapeDtypeStruct((TOK, HEAD_DIM), BF16),
            jax.ShapeDtypeStruct((4, 512), F32),
        ),
        in_specs=[hbm] * 6,
        out_specs=(vmem, vmem, vmem),
        scratch_shapes=[
            pltpu.SMEM((16,), F32),
            pltpu.SMEM((2,), jnp.int32),
            pltpu.VMEM((4, 512), BF16),
            pltpu.VMEM((16, 128), F32),
            blocks(),
            blocks(4, 8), blocks(8, 4),
            pltpu.VMEM((128, 128), F32),
            pltpu.VMEM((128, 512), BF16),
            pltpu.VMEM((128, 512), BF16),
            pltpu.VMEM((2, 2048, 128), BF16),
            pltpu.VMEM((2048, 128), F32),
            pltpu.VMEM((2, 512, 512), BF16),
            pltpu.VMEM((2, 512, 512), BF16),
            tok, tok, tok, tok_t, tok_t, tok_t, tok_t,
            pltpu.VMEM((8, 32, 256), F32),
            pltpu.VMEM((8, 32, 256), F32),
            tile8, tile8, tile8, tile8,
            pltpu.VMEM((2, 512, 128), F32),
            blocks(4, 8), blocks(8, 4),
            blocks(8, 8), blocks(8, 4),
            blocks(8), blocks(4), blocks(8),
            dma((6,)),
        ] + [dma] * 24,
        compiler_params=pltpu.CompilerParams(
            collective_id=0, has_side_effects=True, vmem_limit_bytes=20 * 1024 * 1024
        ),
        name="cross_attention",
    )(*(
        pltpu.with_memory_space_constraint(a, pltpu.HBM)
        for a in (
            vision_states,
            projection.reshape(2048, 128),
            queries.reshape(TOK, HEAD_DIM),
            cotangent.reshape(TOK, HEAD_DIM),
            gate_logit,
            tile_counts,
        )
    ))
    return (
        attended.reshape(queries.shape),
        query_grad.reshape(queries.shape),
        image_grad,
    )


def solution(mesh):
    return jax.shard_map(
        on_device,
        mesh=mesh,
        in_specs=(
            P("section", "tensor"),
            P("section", "tensor", None, None, None),
            P("section", None, "tensor"),
            P("section", None, "tensor"),
            P(),
            P(),
        ),
        out_specs=(
            P("section", None, "tensor"),
            P("section", None, "tensor"),
            P("section", "tensor"),
        ),
        check_vma=False,
    )
```

```python
import jax
import jax.numpy as jnp
from jax import lax
from jax.experimental import pallas as pl
from jax.experimental.pallas import tpu as pltpu
from jax.sharding import PartitionSpec as P

MESH = pl.DeviceIdType.MESH
BF16 = jnp.bfloat16
F32 = jnp.float32

HEAD_DIM = 128
GROUPS = 4
TILE_ROWS = 32
TILES = 4
SCALE = HEAD_DIM ** (-0.5)
TOK = 2048
SAMPLE_TOK = 1024
CHUNK = 512
SIDE = 8
FAR_FIRST = (4, 3, 5, 2, 6, 1, 7)


def arrived(ref, sem):
    pltpu.make_async_copy(ref, ref, sem).wait()


def kernel(
    vis_ref, w_ref, q_ref, cot_ref, gate_ref, count_ref,
    att_ref, qg_ref, img_ref,
    gate_s, count_s, vis_v, msg_f, msg, vin_a, vin_b, vf, vb_a, vb_b, w_raw, w_f, w_cat, w_t,
    q_v, cot_v, gi_v, q_t, gi_t, probs_s, ds_s,
    part, r1, kv, grads, r2, r3, g_f, e_msg, r4,
    load_sem, w_send, w_recv, a1_send, a1a_recv, a1b_recv, a2a_send, a2b_send, a2a_recv, a2b_recv,
    b1_send, b1_recv, b2_send, b2_recv, d1_send, d1_recv, d2_send, d2_recv,
    e_send, e_recv, ready,
):
    sec = lax.axis_index("section")
    ten = lax.axis_index("tensor")
    x, y = sec // SIDE, sec % SIDE
    z, core = ten // 2, ten % 2
    sample = x // 4
    half = z // 4
    tile = x % 4
    sum_tile = z % 4
    slot = ten % 8
    is_own = core == sample

    def chip(cx, cy, c):
        return (cx * SIDE + cy, z * 2 + c)

    def tensor_peer(t):
        return (sec, t)

    def remote(src, dst, send, recv, device):
        return pltpu.make_async_remote_copy(
            src_ref=src, dst_ref=dst, send_sem=send, recv_sem=recv,
            device_id=device, device_id_type=MESH,
        )

    load_v = pltpu.make_async_copy(vis_ref, vis_v, load_sem.at[3])
    load_q = pltpu.make_async_copy(q_ref, q_v, load_sem.at[0])
    load_c = pltpu.make_async_copy(cot_ref, cot_v, load_sem.at[1])
    load_w = pltpu.make_async_copy(w_ref, w_raw.at[core], load_sem.at[2])
    load_g = pltpu.make_async_copy(gate_ref, gate_s, load_sem.at[4])
    load_n = pltpu.make_async_copy(count_ref, count_s, load_sem.at[5])
    load_v.start()
    load_g.start()
    load_n.start()
    load_w.start()
    load_c.start()
    load_q.start()

    barrier = pltpu.get_barrier_semaphore()

    def greet(device):
        pl.semaphore_signal(barrier, inc=1, device_id=device, device_id_type=MESH)

    for d in FAR_FIRST:
        for c in range(2):
            greet(chip((x + d) % SIDE, y, c))
            greet(chip(x, (y + d) % SIDE, c))
    for i in range(8):
        @pl.when(jnp.logical_and(i // 2 >= sum_tile, i != slot))
        def _():
            greet(tensor_peer(half * 8 + i))

    @pl.when(half == 0)
    def _():
        for i in range(4):
            greet(tensor_peer((4 + i) * 2 + core))

    load_v.wait()
    for k in range(4):
        msg_f[4 * k : 4 * k + 4, :] = vis_v[:, 128 * k : 128 * (k + 1)].astype(F32)
    msg[...] = msg_f[...].astype(BF16)

    pl.semaphore_wait(barrier, 29 + 2 * sum_tile + 4 * half)

    @pl.when(core == 0)
    def _():
        for d in FAR_FIRST:
            remote(msg, vin_a.at[tile, y], a1_send, a1a_recv, chip(x, (y + d) % SIDE, sample)).start()

        @pl.when(is_own)
        def _():
            pltpu.make_async_copy(msg, vin_a.at[tile, y], a1a_recv).start()

        @pl.when(jnp.logical_not(is_own))
        def _():
            remote(msg, vin_a.at[tile, y], a1_send, a1a_recv, chip(x, y, 1)).start()

    @pl.when(core == 1)
    def _():
        for d in FAR_FIRST:
            remote(msg, vin_b.at[y, tile], a1_send, a1b_recv, chip((x + d) % SIDE, y, sample)).start()

        @pl.when(is_own)
        def _():
            pltpu.make_async_copy(msg, vin_b.at[y, tile], a1b_recv).start()

        @pl.when(jnp.logical_not(is_own))
        def _():
            remote(msg, vin_b.at[y, tile], a1_send, a1b_recv, chip(x, y, 0)).start()

    for i in range(6):
        @pl.when(i // 2 < sum_tile)
        def _():
            pl.semaphore_signal(
                ready, inc=1, device_id=tensor_peer(half * 8 + i), device_id_type=MESH
            )

    @pl.when(half == 1)
    def _():
        for i in range(4):
            pl.semaphore_signal(
                ready, inc=1, device_id=tensor_peer(i * 2 + core), device_id_type=MESH
            )

    def lay_out(m):
        w_f[...] = w_raw[m].astype(F32)
        for n in range(4):
            block = w_f[pl.ds(n, 512, stride=4), :]
            w_cat[m, :, 128 * n : 128 * (n + 1)] = block.astype(BF16)
            w_t[m, 128 * n : 128 * (n + 1), :] = block.T.astype(BF16)

    load_w.wait()
    lay_out(core)

    arrived(vin_b.at[y], a1b_recv)
    for d in FAR_FIRST:
        remote(vin_b.at[y], vin_b.at[y], a2b_send, a2b_recv, chip(x, (y + d) % SIDE, core)).start()

    @pl.when(is_own)
    def _():
        arrived(vin_a.at[tile], a1a_recv)
        for d in FAR_FIRST:
            remote(vin_a.at[tile], vin_a.at[tile], a2a_send, a2a_recv, chip((x + d) % SIDE, y, core)).start()

    w_copy = remote(w_ref, w_raw.at[core], w_send, w_recv, tensor_peer(z * 2 + 1 - core))
    w_copy.start()
    load_g.wait()
    load_n.wait()
    gate = jnp.tanh(jnp.full((8, 128), gate_s[sec // GROUPS], F32))[0:1, 0:1]
    w_copy.wait_recv()
    lay_out(1 - core)
    load_c.wait()
    load_q.wait()
    for t in range(TOK // CHUNK):
        rows = slice(t * CHUNK, (t + 1) * CHUNK)
        gi = (gate * cot_v[rows, :].astype(F32)).astype(BF16)
        gi_v[rows, :] = gi
        gi_t[:, rows] = gi.astype(F32).T.astype(BF16)
        q_t[:, rows] = q_v[rows, :].astype(F32).T.astype(BF16)

    def rows_of(blocks, out):
        for j in range(TILES):
            vf[...] = blocks(j).reshape(128, 128).astype(F32)
            for k in range(4):
                rows = [vf[pl.ds(4 * k + r, 8, stride=16), :] for r in range(4)]
                out[32 * j : 32 * (j + 1), 128 * k : 128 * (k + 1)] = jnp.concatenate(
                    rows, axis=0
                ).astype(BF16)

    arrived(vin_b.at[pl.ds(0, 7)], a2b_recv)
    rows_of(lambda j: vin_b[:, j], vb_b)

    @pl.when(is_own)
    def _():
        arrived(vin_a.at[pl.ds(0, 3)], a2a_recv)

    @pl.when(jnp.logical_not(is_own))
    def _():
        arrived(vin_a, a2a_recv)

    rows_of(lambda j: vin_a[j], vb_a)
    total = jnp.dot(vb_a[...], w_cat[0], preferred_element_type=F32) + jnp.dot(
        vb_b[...], w_cat[1], preferred_element_type=F32
    )
    for g in range(2):
        part[4 * g : 4 * g + 4] = total[:, 256 * g : 256 * (g + 1)].reshape(4, 32, 256)

    @pl.when(z < SIDE - 1)
    def _():
        pl.semaphore_wait(ready, 2 * (3 - sum_tile) + 4 * (1 - half))

    for d in FAR_FIRST:
        dest = (z + d) % 8
        remote(part.at[dest], r1.at[z], b1_send, b1_recv, tensor_peer(dest * 2 + core)).start()

    arrived(r1.at[pl.ds(0, 7)], b1_recv)
    total = part[z]
    for i in range(1, 8):
        total = total + r1[(z + i) % 8]
    kv_slot = core * 4 + sum_tile
    kv[kv_slot] = total.astype(BF16)

    for i in range(1, 8):
        remote(
            kv.at[kv_slot], kv.at[kv_slot], b2_send, b2_recv,
            tensor_peer(half * 8 + (slot + i) % 8),
        ).start()
    arrived(kv.at[pl.ds(0, 7)], b2_recv)

    row_tile = lax.broadcasted_iota(jnp.int32, (128, CHUNK), 0) // TILE_ROWS
    for b in range(2):
        both = kv[4 * b : 4 * b + 4].reshape(128, 256)
        keys, values = both[:, :128], both[:, 128:]
        usable = row_tile < count_s[b]
        key_grad = jnp.zeros((128, HEAD_DIM), F32)
        value_grad = jnp.zeros((128, HEAD_DIM), F32)
        for t in range(SAMPLE_TOK // CHUNK):
            rows = slice(b * SAMPLE_TOK + t * CHUNK, b * SAMPLE_TOK + (t + 1) * CHUNK)
            scores = jnp.dot(keys, q_t[:, rows], preferred_element_type=F32) * SCALE
            masked = jnp.where(usable, scores, -1e30)
            row_max = jnp.max(masked, axis=0, keepdims=True)
            weights = jnp.where(usable, jnp.exp(masked - row_max), 0.0)
            probs = weights * (1.0 / jnp.sum(weights, axis=0, keepdims=True))
            probs_low = probs.astype(BF16)
            grad_probs = jnp.dot(values, gi_t[:, rows], preferred_element_type=F32)
            center = jnp.sum(probs * grad_probs, axis=0, keepdims=True)
            grad_scores = (probs * (grad_probs - center)).astype(BF16)
            key_grad = key_grad + jnp.dot(grad_scores, q_v[rows, :], preferred_element_type=F32)
            value_grad = value_grad + jnp.dot(probs_low, gi_v[rows, :], preferred_element_type=F32)
            probs_s[:, rows] = probs_low
            ds_s[:, rows] = grad_scores
        part_grads = jnp.concatenate([(key_grad * SCALE).astype(BF16), value_grad.astype(BF16)], axis=1)
        grads[4 * b : 4 * b + 4] = part_grads.reshape(4, 32, 256)

        for j in range(TILES):
            dest = j * 2 + b

            @pl.when(dest != slot)
            def _():
                remote(
                    grads.at[4 * b + j], r2.at[slot], d1_send, d1_recv, tensor_peer(half * 8 + dest)
                ).start()

    def outputs(b):
        both = kv[4 * b : 4 * b + 4].reshape(128, 256).astype(F32)
        keys_t, values_t = both[:, :128].T.astype(BF16), both[:, 128:].T.astype(BF16)
        for t in range(SAMPLE_TOK // CHUNK):
            rows = slice(b * SAMPLE_TOK + t * CHUNK, b * SAMPLE_TOK + (t + 1) * CHUNK)
            combined = jnp.dot(values_t, probs_s[:, rows], preferred_element_type=F32)
            att_ref[rows, :] = (gate * combined).T.astype(BF16)
            query_grad = jnp.dot(keys_t, ds_s[:, rows], preferred_element_type=F32) * SCALE
            qg_ref[rows, :] = query_grad.T.astype(BF16)

    outputs(0)
    arrived(r2.at[pl.ds(0, 7)], d1_recv)
    total = grads[kv_slot].astype(F32)
    for i in range(1, 8):
        total = total + r2[(slot + i) % 8].astype(F32)
    r3[z] = total.astype(BF16)

    for d in FAR_FIRST:
        remote(
            r3.at[z], r3.at[z], d2_send, d2_recv, tensor_peer(((z + d) % 8) * 2 + core)
        ).start()
    outputs(1)
    arrived(r3.at[pl.ds(0, 7)], d2_recv)

    sums = jnp.concatenate([r3[0:4].reshape(128, 256), r3[4:8].reshape(128, 256)], axis=1)
    for m in range(2):
        grad = jnp.dot(sums, w_t[m], preferred_element_type=F32)
        for j in range(TILES):
            for k in range(4):
                for r in range(4):
                    g_f[pl.ds(256 * j + 16 * m + 4 * k + r, 8, stride=32), :] = grad[
                        32 * j + 8 * r : 32 * j + 8 * (r + 1), 128 * k : 128 * (k + 1)
                    ]
    e_msg[...] = g_f[...].astype(BF16).reshape(4, 8, 2, 16, 128)
    for i in range(4):
        j = (tile + 2 + i) % 4
        for d in FAR_FIRST:
            ty = (y + d) % SIDE
            for m in range(2):
                remote(
                    e_msg.at[j, ty, m], r4.at[sec], e_send, e_recv, chip(4 * core + j, ty, m)
                ).start()
        for m in range(2):
            me = jnp.logical_and(is_own, jnp.logical_and(j == tile, core == m))

            @pl.when(me)
            def _():
                pltpu.make_async_copy(e_msg.at[j, y, m], r4.at[sec], e_recv).start()

            @pl.when(jnp.logical_not(me))
            def _():
                remote(
                    e_msg.at[j, y, m], r4.at[sec], e_send, e_recv, chip(4 * core + j, y, m)
                ).start()

    w_copy.wait_send()
    arrived(vin_b.at[pl.ds(0, 7)], a2b_send)
    arrived(part.at[pl.ds(0, 7)], b1_send)
    arrived(kv.at[pl.ds(0, 7)], b2_send)
    arrived(grads.at[pl.ds(0, 7)], d1_send)
    arrived(r3.at[pl.ds(0, 7)], d2_send)

    @pl.when(is_own)
    def _():
        arrived(vin_a.at[0, pl.ds(0, 7)], a1_send)
        arrived(r4.at[pl.ds(0, 56)], a2a_send)
        arrived(r4.at[pl.ds(0, 63)], e_send)

    @pl.when(jnp.logical_not(is_own))
    def _():
        arrived(vin_a.at[0], a1_send)
        arrived(r4, e_send)

    arrived(r4, e_recv)
    image = jnp.sum(r4[...].astype(F32), axis=0)
    for k in range(4):
        img_ref[:, 128 * k : 128 * (k + 1)] = image[4 * k : 4 * k + 4, :]


def copy_out(att_v, qg_v, img_v, att_ref, qg_ref, img_ref, sem):
    copies = [pltpu.make_async_copy(img_v, img_ref, sem.at[8])]
    for i in range(4):
        rows = pl.ds(i * (TOK // 4), TOK // 4)
        copies.append(pltpu.make_async_copy(att_v.at[rows], att_ref.at[rows], sem.at[i]))
        copies.append(pltpu.make_async_copy(qg_v.at[rows], qg_ref.at[rows], sem.at[4 + i]))
    for copy in copies:
        copy.start()
    for copy in copies:
        copy.wait()


def on_device(vision_states, projection, queries, cotangent, gate_logit, tile_counts):
    vmem = pl.BlockSpec(memory_space=pltpu.VMEM)
    hbm = pl.BlockSpec(memory_space=pltpu.HBM)
    dma = pltpu.SemaphoreType.DMA
    tile8 = pltpu.VMEM((8, 32, 256), BF16)
    tok = pltpu.VMEM((TOK, HEAD_DIM), BF16)
    tok_t = pltpu.VMEM((HEAD_DIM, TOK), BF16)

    def blocks(*lead):
        return pltpu.VMEM((*lead, 16, 128), BF16)

    attended, query_grad, image_grad = pl.pallas_call(
        kernel,
        out_shape=(
            jax.ShapeDtypeStruct((TOK, HEAD_DIM), BF16),
            jax.ShapeDtypeStruct((TOK, HEAD_DIM), BF16),
            jax.ShapeDtypeStruct((4, 512), F32),
        ),
        in_specs=[hbm] * 6,
        out_specs=(vmem, vmem, vmem),
        scratch_shapes=[
            pltpu.SMEM((16,), F32),
            pltpu.SMEM((2,), jnp.int32),
            pltpu.VMEM((4, 512), BF16),
            pltpu.VMEM((16, 128), F32),
            blocks(),
            blocks(4, 8), blocks(8, 4),
            pltpu.VMEM((128, 128), F32),
            pltpu.VMEM((128, 512), BF16),
            pltpu.VMEM((128, 512), BF16),
            pltpu.VMEM((2, 2048, 128), BF16),
            pltpu.VMEM((2048, 128), F32),
            pltpu.VMEM((2, 512, 512), BF16),
            pltpu.VMEM((2, 512, 512), BF16),
            tok, tok, tok, tok_t, tok_t, tok_t, tok_t,
            pltpu.VMEM((8, 32, 256), F32),
            pltpu.VMEM((8, 32, 256), F32),
            tile8, tile8, tile8, tile8,
            pltpu.VMEM((1024, 128), F32),
            blocks(4, 8, 2), blocks(64),
            dma((6,)),
        ] + [dma] * 19 + [pltpu.SemaphoreType.REGULAR],
        compiler_params=pltpu.CompilerParams(
            collective_id=0, has_side_effects=True, vmem_limit_bytes=20 * 1024 * 1024
        ),
        name="cross_attention",
    )(*(
        pltpu.with_memory_space_constraint(a, pltpu.HBM)
        for a in (
            vision_states,
            projection.reshape(2048, 128),
            queries.reshape(TOK, HEAD_DIM),
            cotangent.reshape(TOK, HEAD_DIM),
            gate_logit,
            tile_counts,
        )
    ))
    results = (attended, query_grad, image_grad)
    attended, query_grad, image_grad = pl.pallas_call(
        copy_out,
        out_shape=tuple(jax.ShapeDtypeStruct(a.shape, a.dtype) for a in results),
        in_specs=[pl.BlockSpec(memory_space=pl.ANY)] * 3,
        out_specs=(hbm,) * 3,
        scratch_shapes=[dma((9,))],
        compiler_params=pltpu.CompilerParams(vmem_limit_bytes=1024 * 1024),
        name="copy_out",
    )(*results)
    return (
        attended.reshape(queries.shape),
        query_grad.reshape(queries.shape),
        image_grad,
    )


def solution(mesh):
    return jax.shard_map(
        on_device,
        mesh=mesh,
        in_specs=(
            P("section", "tensor"),
            P("section", "tensor", None, None, None),
            P("section", None, "tensor"),
            P("section", None, "tensor"),
            P(),
            P(),
        ),
        out_specs=(
            P("section", None, "tensor"),
            P("section", None, "tensor"),
            P("section", "tensor"),
        ),
        check_vma=False,
    )
```

```python
import jax
import jax.numpy as jnp
from jax import lax
from jax.experimental import pallas as pl
from jax.experimental.pallas import tpu as pltpu
from jax.sharding import PartitionSpec as P

MESH = pl.DeviceIdType.MESH
BF16 = jnp.bfloat16
F32 = jnp.float32

HEAD_DIM = 128
GROUPS = 4
TILE_ROWS = 32
TILES = 4
SCALE = HEAD_DIM ** (-0.5)
TOK = 2048
SAMPLE_TOK = 1024
CHUNK = 512
SIDE = 8
FAR_FIRST = (4, 3, 5, 2, 6, 1, 7)


def arrived(ref, sem):
    pltpu.make_async_copy(ref, ref, sem).wait()


def kernel(
    vis_ref, w_ref, q_ref, cot_ref, gate_ref, count_ref,
    att_ref, qg_ref, img_ref,
    gate_s, count_s, vis_v, msg_f, msg, vin_a, vin_b, vf, vb_a, vb_b, w_raw, w_f, w_cat, w_t,
    q_v, cot_v, gi_v, q_t, gi_t, probs_s, ds_s,
    part, r1, kv, grads, r2, r3, g_f, e_msg, r4,
    load_sem, w_send, w_recv, a1_send, a1a_recv, a1b_recv, a2a_send, a2b_send, a2a_recv, a2b_recv,
    b1_send, b1_recv, b2_send, b2_recv, d1_send, d1_recv, d2_send, d2_recv,
    e_send, e_recv, ready,
):
    sec = lax.axis_index("section")
    ten = lax.axis_index("tensor")
    x, y = sec // SIDE, sec % SIDE
    z, core = ten // 2, ten % 2
    sample = x // 4
    half = z // 4
    tile = x % 4
    sum_tile = z % 4
    slot = ten % 8
    is_own = core == sample

    def chip(cx, cy, c):
        return (cx * SIDE + cy, z * 2 + c)

    def tensor_peer(t):
        return (sec, t)

    def remote(src, dst, send, recv, device):
        return pltpu.make_async_remote_copy(
            src_ref=src, dst_ref=dst, send_sem=send, recv_sem=recv,
            device_id=device, device_id_type=MESH,
        )

    load_v = pltpu.make_async_copy(vis_ref, vis_v, load_sem.at[3])
    load_q = pltpu.make_async_copy(q_ref, q_v, load_sem.at[0])
    load_c = pltpu.make_async_copy(cot_ref, cot_v, load_sem.at[1])
    load_w = pltpu.make_async_copy(w_ref, w_raw.at[core], load_sem.at[2])
    load_g = pltpu.make_async_copy(gate_ref, gate_s, load_sem.at[4])
    load_n = pltpu.make_async_copy(count_ref, count_s, load_sem.at[5])
    load_v.start()
    load_g.start()
    load_n.start()
    load_w.start()
    load_c.start()
    load_q.start()

    barrier = pltpu.get_barrier_semaphore()

    def greet(device):
        pl.semaphore_signal(barrier, inc=1, device_id=device, device_id_type=MESH)

    for d in FAR_FIRST:
        for c in range(2):
            greet(chip((x + d) % SIDE, y, c))
            greet(chip(x, (y + d) % SIDE, c))
    for i in range(8):
        @pl.when(jnp.logical_and(i // 2 >= sum_tile, i != slot))
        def _():
            greet(tensor_peer(half * 8 + i))

    @pl.when(half == 0)
    def _():
        for i in range(4):
            greet(tensor_peer((4 + i) * 2 + core))

    load_v.wait()
    for k in range(4):
        msg_f[4 * k : 4 * k + 4, :] = vis_v[:, 128 * k : 128 * (k + 1)].astype(F32)
    msg[...] = msg_f[...].astype(BF16)

    pl.semaphore_wait(barrier, 29 + 2 * sum_tile + 4 * half)

    @pl.when(core == 0)
    def _():
        for d in FAR_FIRST:
            remote(msg, vin_a.at[tile, y], a1_send, a1a_recv, chip(x, (y + d) % SIDE, sample)).start()

        @pl.when(is_own)
        def _():
            pltpu.make_async_copy(msg, vin_a.at[tile, y], a1a_recv).start()

        @pl.when(jnp.logical_not(is_own))
        def _():
            remote(msg, vin_a.at[tile, y], a1_send, a1a_recv, chip(x, y, 1)).start()

    @pl.when(core == 1)
    def _():
        for d in FAR_FIRST:
            remote(msg, vin_b.at[y, tile], a1_send, a1b_recv, chip((x + d) % SIDE, y, sample)).start()

        @pl.when(is_own)
        def _():
            pltpu.make_async_copy(msg, vin_b.at[y, tile], a1b_recv).start()

        @pl.when(jnp.logical_not(is_own))
        def _():
            remote(msg, vin_b.at[y, tile], a1_send, a1b_recv, chip(x, y, 0)).start()

    for i in range(6):
        @pl.when(i // 2 < sum_tile)
        def _():
            pl.semaphore_signal(
                ready, inc=1, device_id=tensor_peer(half * 8 + i), device_id_type=MESH
            )

    @pl.when(half == 1)
    def _():
        for i in range(4):
            pl.semaphore_signal(
                ready, inc=1, device_id=tensor_peer(i * 2 + core), device_id_type=MESH
            )

    def lay_out(m):
        w_f[...] = w_raw[m].astype(F32)
        for n in range(4):
            block = w_f[pl.ds(n, 512, stride=4), :]
            w_cat[m, :, 128 * n : 128 * (n + 1)] = block.astype(BF16)
            w_t[m, 128 * n : 128 * (n + 1), :] = block.T.astype(BF16)

    load_w.wait()
    lay_out(core)

    arrived(vin_b.at[y], a1b_recv)
    for d in FAR_FIRST:
        remote(vin_b.at[y], vin_b.at[y], a2b_send, a2b_recv, chip(x, (y + d) % SIDE, core)).start()

    @pl.when(is_own)
    def _():
        arrived(vin_a.at[tile], a1a_recv)
        for d in FAR_FIRST:
            remote(vin_a.at[tile], vin_a.at[tile], a2a_send, a2a_recv, chip((x + d) % SIDE, y, core)).start()

    w_copy = remote(w_ref, w_raw.at[core], w_send, w_recv, tensor_peer(z * 2 + 1 - core))
    w_copy.start()
    load_g.wait()
    load_n.wait()
    gate = jnp.tanh(jnp.full((8, 128), gate_s[sec // GROUPS], F32))[0:1, 0:1]
    w_copy.wait_recv()
    lay_out(1 - core)
    load_c.wait()
    load_q.wait()
    for t in range(TOK // CHUNK):
        rows = slice(t * CHUNK, (t + 1) * CHUNK)
        gi = (gate * cot_v[rows, :].astype(F32)).astype(BF16)
        gi_v[rows, :] = gi
        gi_t[:, rows] = gi.astype(F32).T.astype(BF16)
        q_t[:, rows] = q_v[rows, :].astype(F32).T.astype(BF16)

    def rows_of(blocks, out):
        for j in range(TILES):
            vf[...] = blocks(j).reshape(128, 128).astype(F32)
            for k in range(4):
                rows = [vf[pl.ds(4 * k + r, 8, stride=16), :] for r in range(4)]
                out[32 * j : 32 * (j + 1), 128 * k : 128 * (k + 1)] = jnp.concatenate(
                    rows, axis=0
                ).astype(BF16)

    arrived(vin_b.at[pl.ds(0, 7)], a2b_recv)
    rows_of(lambda j: vin_b[:, j], vb_b)

    @pl.when(is_own)
    def _():
        arrived(vin_a.at[pl.ds(0, 3)], a2a_recv)

    @pl.when(jnp.logical_not(is_own))
    def _():
        arrived(vin_a, a2a_recv)

    rows_of(lambda j: vin_a[j], vb_a)
    total = jnp.dot(vb_a[...], w_cat[0], preferred_element_type=F32) + jnp.dot(
        vb_b[...], w_cat[1], preferred_element_type=F32
    )
    for g in range(2):
        part[4 * g : 4 * g + 4] = total[:, 256 * g : 256 * (g + 1)].reshape(4, 32, 256)

    @pl.when(z < SIDE - 1)
    def _():
        pl.semaphore_wait(ready, 2 * (3 - sum_tile) + 4 * (1 - half))

    for d in FAR_FIRST:
        dest = (z + d) % 8
        remote(part.at[dest], r1.at[z], b1_send, b1_recv, tensor_peer(dest * 2 + core)).start()

    arrived(r1.at[pl.ds(0, 7)], b1_recv)
    total = part[z]
    for i in range(1, 8):
        total = total + r1[(z + i) % 8]
    kv_slot = core * 4 + sum_tile
    kv[kv_slot] = total.astype(BF16)

    for i in range(1, 8):
        remote(
            kv.at[kv_slot], kv.at[kv_slot], b2_send, b2_recv,
            tensor_peer(half * 8 + (slot + i) % 8),
        ).start()
    arrived(kv.at[pl.ds(0, 7)], b2_recv)

    row_tile = lax.broadcasted_iota(jnp.int32, (128, CHUNK), 0) // TILE_ROWS
    for b in range(2):
        both = kv[4 * b : 4 * b + 4].reshape(128, 256)
        keys, values = both[:, :128], both[:, 128:]
        usable = row_tile < count_s[b]
        key_grad = jnp.zeros((128, HEAD_DIM), F32)
        value_grad = jnp.zeros((128, HEAD_DIM), F32)
        for t in range(SAMPLE_TOK // CHUNK):
            rows = slice(b * SAMPLE_TOK + t * CHUNK, b * SAMPLE_TOK + (t + 1) * CHUNK)
            scores = jnp.dot(keys, q_t[:, rows], preferred_element_type=F32) * SCALE
            masked = jnp.where(usable, scores, -1e30)
            row_max = jnp.max(masked, axis=0, keepdims=True)
            weights = jnp.where(usable, jnp.exp(masked - row_max), 0.0)
            probs = weights * (1.0 / jnp.sum(weights, axis=0, keepdims=True))
            probs_low = probs.astype(BF16)
            grad_probs = jnp.dot(values, gi_t[:, rows], preferred_element_type=F32)
            center = jnp.sum(probs * grad_probs, axis=0, keepdims=True)
            grad_scores = (probs * (grad_probs - center)).astype(BF16)
            key_grad = key_grad + jnp.dot(grad_scores, q_v[rows, :], preferred_element_type=F32)
            value_grad = value_grad + jnp.dot(probs_low, gi_v[rows, :], preferred_element_type=F32)
            probs_s[:, rows] = probs_low
            ds_s[:, rows] = grad_scores
        part_grads = jnp.concatenate([(key_grad * SCALE).astype(BF16), value_grad.astype(BF16)], axis=1)
        grads[4 * b : 4 * b + 4] = part_grads.reshape(4, 32, 256)

        for j in range(TILES):
            dest = j * 2 + b

            @pl.when(dest != slot)
            def _():
                remote(
                    grads.at[4 * b + j], r2.at[slot], d1_send, d1_recv, tensor_peer(half * 8 + dest)
                ).start()

    def outputs(b):
        both = kv[4 * b : 4 * b + 4].reshape(128, 256).astype(F32)
        keys_t, values_t = both[:, :128].T.astype(BF16), both[:, 128:].T.astype(BF16)
        for t in range(SAMPLE_TOK // CHUNK):
            rows = slice(b * SAMPLE_TOK + t * CHUNK, b * SAMPLE_TOK + (t + 1) * CHUNK)
            combined = jnp.dot(values_t, probs_s[:, rows], preferred_element_type=F32)
            att_ref[rows, :] = (gate * combined).T.astype(BF16)
            query_grad = jnp.dot(keys_t, ds_s[:, rows], preferred_element_type=F32) * SCALE
            qg_ref[rows, :] = query_grad.T.astype(BF16)

    outputs(0)
    arrived(r2.at[pl.ds(0, 7)], d1_recv)
    total = grads[kv_slot].astype(F32)
    for i in range(1, 8):
        total = total + r2[(slot + i) % 8].astype(F32)
    r3[z] = total.astype(BF16)

    for d in FAR_FIRST:
        remote(
            r3.at[z], r3.at[z], d2_send, d2_recv.at[int(d != 4)],
            tensor_peer(((z + d) % 8) * 2 + core),
        ).start()
    outputs(1)
    def image_rows(steps):
        count = len(steps)
        places = [(sum_tile + step) % 4 for step in steps]
        sums = jnp.concatenate(
            [
                jnp.concatenate([r3[place] for place in places], axis=0),
                jnp.concatenate([r3[4 + place] for place in places], axis=0),
            ],
            axis=1,
        )
        for m in range(2):
            grad = jnp.dot(sums, w_t[m], preferred_element_type=F32)
            for j in range(count):
                for k in range(4):
                    for r in range(4):
                        g_f[pl.ds(256 * steps[j] + 16 * m + 4 * k + r, 8, stride=32), :] = grad[
                            32 * j + 8 * r : 32 * j + 8 * (r + 1), 128 * k : 128 * (k + 1)
                        ]
        low = steps[0]
        e_msg[low : low + count] = (
            g_f[256 * low : 256 * (low + count), :].astype(BF16).reshape(count, 8, 2, 16, 128)
        )

    def send_rows(step):
        j = (sum_tile + step) % 4
        for d in FAR_FIRST:
            ty = (y + d) % SIDE
            for m in range(2):
                remote(
                    e_msg.at[step, ty, m], r4.at[sec], e_send, e_recv, chip(4 * core + j, ty, m)
                ).start()
        for m in range(2):
            me = jnp.logical_and(is_own, jnp.logical_and(j == tile, core == m))

            @pl.when(me)
            def _():
                pltpu.make_async_copy(e_msg.at[step, y, m], r4.at[sec], e_recv).start()

            @pl.when(jnp.logical_not(me))
            def _():
                remote(
                    e_msg.at[step, y, m], r4.at[sec], e_send, e_recv, chip(4 * core + j, y, m)
                ).start()

    arrived(r3.at[pl.ds(0, 6)], d2_recv.at[1])
    image_rows((1, 2, 3))
    for i in range(3):
        send_rows(1 + (tile + i) % 3)
    arrived(r3.at[0], d2_recv.at[0])
    image_rows((0,))
    send_rows(0)

    w_copy.wait_send()
    arrived(vin_b.at[pl.ds(0, 7)], a2b_send)
    arrived(part.at[pl.ds(0, 7)], b1_send)
    arrived(kv.at[pl.ds(0, 7)], b2_send)
    arrived(grads.at[pl.ds(0, 7)], d1_send)
    arrived(r3.at[pl.ds(0, 7)], d2_send)

    @pl.when(is_own)
    def _():
        arrived(vin_a.at[0, pl.ds(0, 7)], a1_send)
        arrived(r4.at[pl.ds(0, 56)], a2a_send)
        arrived(r4.at[pl.ds(0, 63)], e_send)

    @pl.when(jnp.logical_not(is_own))
    def _():
        arrived(vin_a.at[0], a1_send)
        arrived(r4, e_send)

    arrived(r4, e_recv)
    image = jnp.sum(r4[...].astype(F32), axis=0)
    for k in range(4):
        img_ref[:, 128 * k : 128 * (k + 1)] = image[4 * k : 4 * k + 4, :]


def copy_out(att_v, qg_v, img_v, att_ref, qg_ref, img_ref, sem):
    copies = [pltpu.make_async_copy(img_v, img_ref, sem.at[8])]
    for i in range(4):
        rows = pl.ds(i * (TOK // 4), TOK // 4)
        copies.append(pltpu.make_async_copy(att_v.at[rows], att_ref.at[rows], sem.at[i]))
        copies.append(pltpu.make_async_copy(qg_v.at[rows], qg_ref.at[rows], sem.at[4 + i]))
    for copy in copies:
        copy.start()
    for copy in copies:
        copy.wait()


def on_device(vision_states, projection, queries, cotangent, gate_logit, tile_counts):
    vmem = pl.BlockSpec(memory_space=pltpu.VMEM)
    hbm = pl.BlockSpec(memory_space=pltpu.HBM)
    dma = pltpu.SemaphoreType.DMA
    tile8 = pltpu.VMEM((8, 32, 256), BF16)
    tok = pltpu.VMEM((TOK, HEAD_DIM), BF16)
    tok_t = pltpu.VMEM((HEAD_DIM, TOK), BF16)

    def blocks(*lead):
        return pltpu.VMEM((*lead, 16, 128), BF16)

    attended, query_grad, image_grad = pl.pallas_call(
        kernel,
        out_shape=(
            jax.ShapeDtypeStruct((TOK, HEAD_DIM), BF16),
            jax.ShapeDtypeStruct((TOK, HEAD_DIM), BF16),
            jax.ShapeDtypeStruct((4, 512), F32),
        ),
        in_specs=[hbm] * 6,
        out_specs=(vmem, vmem, vmem),
        scratch_shapes=[
            pltpu.SMEM((16,), F32),
            pltpu.SMEM((2,), jnp.int32),
            pltpu.VMEM((4, 512), BF16),
            pltpu.VMEM((16, 128), F32),
            blocks(),
            blocks(4, 8), blocks(8, 4),
            pltpu.VMEM((128, 128), F32),
            pltpu.VMEM((128, 512), BF16),
            pltpu.VMEM((128, 512), BF16),
            pltpu.VMEM((2, 2048, 128), BF16),
            pltpu.VMEM((2048, 128), F32),
            pltpu.VMEM((2, 512, 512), BF16),
            pltpu.VMEM((2, 512, 512), BF16),
            tok, tok, tok, tok_t, tok_t, tok_t, tok_t,
            pltpu.VMEM((8, 32, 256), F32),
            pltpu.VMEM((8, 32, 256), F32),
            tile8, tile8, tile8, tile8,
            pltpu.VMEM((1024, 128), F32),
            blocks(4, 8, 2), blocks(64),
            dma((6,)),
        ] + [dma] * 16 + [dma((2,))] + [dma] * 2 + [pltpu.SemaphoreType.REGULAR],
        compiler_params=pltpu.CompilerParams(
            collective_id=0, has_side_effects=True, vmem_limit_bytes=20 * 1024 * 1024
        ),
        name="cross_attention",
    )(*(
        pltpu.with_memory_space_constraint(a, pltpu.HBM)
        for a in (
            vision_states,
            projection.reshape(2048, 128),
            queries.reshape(TOK, HEAD_DIM),
            cotangent.reshape(TOK, HEAD_DIM),
            gate_logit,
            tile_counts,
        )
    ))
    results = (attended, query_grad, image_grad)
    attended, query_grad, image_grad = pl.pallas_call(
        copy_out,
        out_shape=tuple(jax.ShapeDtypeStruct(a.shape, a.dtype) for a in results),
        in_specs=[pl.BlockSpec(memory_space=pl.ANY)] * 3,
        out_specs=(hbm,) * 3,
        scratch_shapes=[dma((9,))],
        compiler_params=pltpu.CompilerParams(vmem_limit_bytes=1024 * 1024),
        name="copy_out",
    )(*results)
    return (
        attended.reshape(queries.shape),
        query_grad.reshape(queries.shape),
        image_grad,
    )


def solution(mesh):
    return jax.shard_map(
        on_device,
        mesh=mesh,
        in_specs=(
            P("section", "tensor"),
            P("section", "tensor", None, None, None),
            P("section", None, "tensor"),
            P("section", None, "tensor"),
            P(),
            P(),
        ),
        out_specs=(
            P("section", None, "tensor"),
            P("section", None, "tensor"),
            P("section", "tensor"),
        ),
        check_vma=False,
    )
```
